512 devices in a mesh: energy: 128 (over z, y, core), transpor: 4 (over x).
Axes of the slice: x: 4, y: 8, z: 8, core: 2. Of those that a mesh axis runs over, the one named last changes fastest.
Arguments:
- onsite: float32 [4, 128, 128], P('transpor'), may hold values from -1 to 1, as said below
- hopping: float32 [4, 128, 128], P('transpor'), may hold values from -0.25 to 0.25
- selfenergy: float32 [128, 4, 128, 128], P('energy', 'transpor'), may hold values from -1 to 1, as said below
- broadening: float32 [128, 4, 128], P('energy', 'transpor'), may hold values from 0.1 to 0.5
Outputs:
- green: float32 [128, 2, 4, 128, 128], P('energy', None, 'transpor')
- polar: float32 [128, 2, 4, 128, 128], P('energy', None, 'transpor')
The draws below stay inside these ranges and needn't reach their ends.
Inputs may be any that keep to these rules, and one draw needn't show every extreme that they name: `onsite`: each block is symmetric. `selfenergy`: each block is symmetric.
All inputs are finite; a program needn't handle non-finite values.
Results may differ from the reference program's by a relative error of at most 0.00021.
Values sent between devices are 32-bit elements; how exact they have to be, the bound alone decides.
A program may use at most 128 MiB of HBM per device.

```python
import math
import jax
import jax.numpy as jnp
from jax import lax

B = 128
NB = 4
NE = 128


def draw_onsite(key, part):
    normal_noise = jax.random.normal(key, (NB, B, B), jnp.float32)
    normal_noise = jnp.clip(normal_noise, -4.0, 4.0)
    symmetric = (normal_noise + jnp.swapaxes(normal_noise, 1, 2)) * (0.35 / math.sqrt(B))
    levels = jax.random.uniform(jax.random.fold_in(key, 7), (NB, B), jnp.float32, -0.4, 0.4)
    return symmetric + levels[:, :, None] * jnp.eye(B, dtype=jnp.float32)


def draw_selfenergy(key, part):
    normal_noise = jax.random.normal(key, (NE, NB, B, B), jnp.float32)
    normal_noise = jnp.clip(normal_noise, -4.0, 4.0)
    return (normal_noise + jnp.swapaxes(normal_noise, 2, 3)) * (0.1 / math.sqrt(B))


def block_scale(stream_key, extent, split, low, largest):
    loudness, own = 1.0, jax.random.fold_in(stream_key, 6)
    for dim, blocks in split:
        steps = jnp.exp(jax.random.uniform(jax.random.fold_in(own, dim), (blocks,), jnp.float32, low / len(split), largest / len(split)))
        loudness = loudness * jnp.repeat(steps, extent[dim] // blocks).reshape([-1 if axis == dim else 1 for axis in range(len(extent))])
    return loudness


def noise(stream_key, dims, deviation, limit, shards=(), kind=jnp.bfloat16):
    result = jax.random.normal(stream_key, dims, jnp.float32) * deviation
    if len(shards) > 0:
        result = block_scale(stream_key, dims, shards, -0.22, 0.18) * result
    return jnp.clip(result, min=-limit, max=limit).astype(kind)


def setup_inputs(seed: int = 0) -> dict:
    splits = jax.random.split(jax.random.key(seed), 5)
    onsite = draw_onsite(jax.random.fold_in(splits[4], 71), 0)
    hopping = noise(splits[1], (NB, B, B), (4 * B) ** -0.5, 0.25, ((0, 4),), jnp.float32)
    selfenergy = draw_selfenergy(jax.random.fold_in(splits[4], 71), 0)
    broadening = jnp.clip(jnp.exp(math.log(0.5) - 1.609438 * jax.random.uniform(splits[3], (NE, NB, B), jnp.float32) ** block_scale(splits[3], (NE, NB, B), ((0, 128), (1, 4)), -0.2, 0.2)), 0.1, 0.5)
    return {"onsite": onsite, "hopping": hopping, "selfenergy": selfenergy, "broadening": broadening}


ENERGY_LOW = -1.5
ENERGY_HIGH = 1.5

def product(left, right):
    return jnp.matmul(left, right, precision=lax.Precision.HIGHEST)

def flipped(matrix):
    return jnp.swapaxes(matrix, -1, -2)

def complex_mul(first, second):
    return (product(first[0], second[0]) - product(first[1], second[1]), product(first[0], second[1]) + product(first[1], second[0]))

def complex_add(first, second):
    return (first[0] + second[0], first[1] + second[1])

def real_left(matrix, value):
    return (product(matrix, value[0]), product(matrix, value[1]))

def real_right(value, matrix):
    return (product(value[0], matrix), product(value[1], matrix))

def invert(value):
    real_part, imag_part = value
    normal_real = product(flipped(real_part), real_part) + product(flipped(imag_part), imag_part)
    normal_imag = product(flipped(real_part), imag_part) - product(flipped(imag_part), real_part)
    upper_rows = jnp.concatenate([normal_real, -normal_imag], -1)
    lower_rows = jnp.concatenate([normal_imag, normal_real], -1)
    factor = jnp.linalg.cholesky(jnp.concatenate([upper_rows, lower_rows], -2))
    target = jnp.concatenate([flipped(real_part), -flipped(imag_part)], -2)
    solved = jax.scipy.linalg.cho_solve((factor, True), target)
    orders = real_part.shape[-1]
    return (solved[..., :orders, :], solved[..., orders:, :])

def direct_sum(values):
    energy_total = values.shape[0]
    padded = jnp.concatenate([jnp.zeros_like(values), values], 0)

    def lagged_sum(shift):
        lagged = lax.dynamic_slice_in_dim(padded, energy_total - shift, energy_total, 0)
        real_sum = jnp.sum(values[:, 0] * lagged[:, 0] + values[:, 1] * lagged[:, 1], 0)
        imag_sum = jnp.sum(values[:, 1] * lagged[:, 0] - values[:, 0] * lagged[:, 1], 0)
        return jnp.stack([real_sum, imag_sum]) / energy_total
    return lax.map(lagged_sum, jnp.arange(energy_total, dtype=jnp.int32))

def reference(onsite, hopping, selfenergy, broadening):
    levels = ENERGY_LOW + (ENERGY_HIGH - ENERGY_LOW) * (jnp.arange(NE, dtype=jnp.int32).astype(jnp.float32) + 0.5) / NE
    unit_matrix = jnp.eye(B, dtype=jnp.float32)
    contact = product(hopping[NB - 1], flipped(hopping[NB - 1]))
    connected = []
    for block_index in range(NB):
        real_part = levels[:, None, None] * unit_matrix - onsite[block_index] - selfenergy[:, block_index]
        imag_part = broadening[:, block_index, :, None] * unit_matrix
        if block_index == NB - 1:
            imag_part = imag_part + contact
        if block_index > 0:
            coupling = hopping[block_index - 1]
            shifted = real_right(real_left(flipped(coupling), connected[-1]), coupling)
            real_part = real_part - shifted[0]
            imag_part = imag_part - shifted[1]
        connected.append(invert((real_part, imag_part)))
    greens = [connected[-1]]
    for block_index in range(NB - 2, -1, -1):
        left_green = connected[block_index]
        coupling = hopping[block_index]
        dressed = real_right(real_left(coupling, greens[0]), flipped(coupling))
        greens.insert(0, complex_add(left_green, complex_mul(left_green, complex_mul(dressed, left_green))))
    green = jnp.stack([jnp.stack([value_pair[0] for value_pair in greens], 1), jnp.stack([value_pair[1] for value_pair in greens], 1)], 1)
    polar = direct_sum(green)
    return (green, polar)
```

```python
import jax
import jax.numpy as jnp
import numpy as np
from jax import lax
from jax.experimental import pallas as pl
from jax.experimental.pallas import tpu as pltpu
from jax.sharding import PartitionSpec as P

N = 128
NB = 8
NE = 128
ENERGY_LOW = -1.5
ENERGY_HIGH = 1.5
MESH = pl.DeviceIdType.MESH
HIGHEST = lax.Precision.HIGHEST
F32 = jnp.float32
BF16 = jnp.bfloat16


def correlation_tables():
    freq = np.arange(NE)[:, None]
    time = np.arange(NE)[None, :]
    angle = 2.0 * np.pi * ((freq * time) % (2 * NE)) / (2 * NE)
    cosine, sine = np.cos(angle), np.sin(angle)
    alternate = np.where(np.arange(NE) % 2 == 0, 1.0, -1.0)
    lower = sine.copy()
    lower[0] = alternate
    forward = np.concatenate([cosine, lower], 0)
    weight = np.full((NE,), 2.0)
    weight[0] = 1.0
    scale = 1.0 / (2 * NE * NE)
    upper_right = np.zeros((NE, NE))
    upper_right[:, 0] = alternate
    backward = scale * np.block([[cosine.T * weight[None, :], upper_right], [np.zeros((NE, NE)), 4.0 * sine.T]])

    def halves(table):
        high = table.astype(np.float32).astype(BF16)
        low = (table - high.astype(np.float64)).astype(np.float32).astype(BF16)
        return high, low

    fh, fl = halves(forward)
    bh, bl = halves(backward)
    return np.concatenate([fh, fh, fl], 1), np.concatenate([bh, bh, bl], 1)


def split2(x):
    high = x.astype(BF16)
    return high, (x - high.astype(F32)).astype(BF16)


def split3(x):
    high = x.astype(BF16).astype(F32)
    rest = x - high
    middle = rest.astype(BF16).astype(F32)
    return high, middle, rest - middle


def mm(a, b, dims=((1,), (0,))):
    return lax.dot_general(a, b, (dims, ((), ())), precision=HIGHEST, preferred_element_type=F32)


def lane_copy(x, column):
    return jnp.broadcast_to(x[:, column : column + 1], (NB, N))


def row_copy(x, row):
    return jnp.broadcast_to(x[row : row + 1, :], (NB, N))


def eliminate(pr, pi, lane, sub, first):
    columns = [(lane_copy(pr, first + j), lane_copy(pi, first + j)) for j in range(NB)]
    for row in range(NB):
        here = sub == row
        cr, ci = columns[row]
        dr, di = row_copy(cr, row), row_copy(ci, row)
        over = 1.0 / (dr * dr + di * di)
        ir, ni = dr * over, di * over
        fr = jnp.where(here, -ir, cr * ir + ci * ni)
        fi = jnp.where(here, ni, ci * ir - cr * ni)

        def step(xr, xi):
            rr, ri = row_copy(xr, row), row_copy(xi, row)
            return (
                jnp.where(here, 0.0, xr) - (fr * rr - fi * ri),
                jnp.where(here, 0.0, xi) - (fr * ri + fi * rr),
            )

        for j in range(row + 1, NB):
            columns[j] = step(*columns[j])
        hit = lane == first + row
        unit = jnp.where(here, 1.0, 0.0)
        pr, pi = step(jnp.where(hit, unit, pr), jnp.where(hit, 0.0, pi))
    return pr, pi


def rank_update(lr, li, wr, wi):
    ls = (split3(lr), split3(li))
    ws = (split3(wr), split3(wi))
    left, right = [], []
    for a, b in ((0, 0), (0, 1), (1, 0), (1, 1), (0, 2), (2, 0)):
        left += [ls[0][a], ls[1][a]]
        right += [
            jnp.concatenate([ws[0][b], ws[1][b]], 1),
            jnp.concatenate([-ws[1][b], ws[0][b]], 1),
        ]
    return lax.dot_general(
        jnp.concatenate(left, 0),
        jnp.concatenate(right, 0),
        (((0,), (0,)), ((), ())),
        precision=lax.Precision.DEFAULT,
        preferred_element_type=F32,
    )


def replace_rows(old, start, new):
    parts = [old[:start]] if start else []
    parts.append(new)
    if start + NB < N:
        parts.append(old[start + NB :])
    return jnp.concatenate(parts, 0)


def invert(mr, mi):
    lane = lax.broadcasted_iota(jnp.int32, (NB, N), 1)
    sub = lax.broadcasted_iota(jnp.int32, (NB, N), 0)
    pr, pi = mr[:NB], mi[:NB]
    for start in range(0, N, NB):
        wr, wi = eliminate(pr, pi, lane, sub, start)
        done = lane < start
        lr, li = jnp.where(done, -pr, pr), jnp.where(done, -pi, pi)
        if start + NB < N:
            active = (lane >= start) & (lane < start + NB)
            sr, si = mr[start + NB : start + 2 * NB], mi[start + NB : start + 2 * NB]
            pr, pi = jnp.where(active, 0.0, sr), jnp.where(active, 0.0, si)
            for j in range(NB):
                cr, ci = lane_copy(sr, start + j), lane_copy(si, start + j)
                xr, xi = row_copy(wr, j), row_copy(wi, j)
                pr = pr - (cr * xr - ci * xi)
                pi = pi - (cr * xi + ci * xr)
        update = rank_update(lr, li, jnp.where(lane == start + sub, wr + 1.0, wr), wi)
        mr = replace_rows(mr - update[:, :N], start, wr)
        mi = replace_rows(mi - update[:, N:], start, wi)
    return mr, mi


def fused(
    onsite,
    hopping,
    selfenergy,
    broadening,
    forward,
    backward,
    green,
    polar,
    real_in,
    side_in,
    diag_in,
    near,
    own,
    far,
    matrix,
    coupling,
    lifted,
    block,
    spread,
    sums,
    forward_table,
    backward_table,
    send_sem,
    recv_sem,
    far_sem,
    table_sem,
    swap_sem,
    green_sem,
    line_sem,
):
    x = lax.axis_index("transpor")
    e = lax.axis_index("energy")
    z, y, c = e // 16, lax.rem(e // 2, 8), lax.rem(e, 2)
    plane = z * 2 + c

    def plane_peer(s):
        i = lax.rem(plane + s, 16)
        return (i // 2) * 16 + y * 2 + lax.rem(i, 2)

    def row_peer(s):
        return z * 16 + lax.rem(y + s, 8) * 2 + c

    barrier = pltpu.get_barrier_semaphore()
    for s in range(1, 4):
        pl.semaphore_signal(barrier, inc=1, device_id={"transpor": lax.rem(x + s, 4)}, device_id_type=MESH)

    @pl.loop(1, 16)
    def _(s):
        pl.semaphore_signal(barrier, inc=1, device_id={"energy": plane_peer(s)}, device_id_type=MESH)

    @pl.loop(1, 8)
    def _(s):
        pl.semaphore_signal(barrier, inc=1, device_id={"energy": row_peer(s)}, device_id_type=MESH)

    tables = [
        pltpu.make_async_copy(forward, forward_table, table_sem.at[0]),
        pltpu.make_async_copy(backward, backward_table, table_sem.at[1]),
    ]
    for copy in tables:
        copy.start()

    level = ENERGY_LOW + (ENERGY_HIGH - ENERGY_LOW) * (e.astype(F32) + 0.5) / NE
    rows = lax.broadcasted_iota(jnp.int32, (N, N), 0)
    lanes = lax.broadcasted_iota(jnp.int32, (N, N), 1)
    unit = rows == lanes

    def diagonal(row):
        return jnp.where(unit, jnp.broadcast_to(row, (N, N)), 0.0)

    real_in[x] = jnp.where(unit, level, 0.0) - onsite[...] - selfenergy[...]
    diag_in[x] = jnp.broadcast_to(broadening[...], (8, N))

    @pl.when(x < 3)
    def _():
        side_in[x] = hopping[...]

    @pl.when(x == 3)
    def _():
        outgoing = hopping[...]
        side_in[x] = diagonal(broadening[...]) + mm(outgoing, outgoing, ((1,), (1,)))

    pl.semaphore_wait(barrier, 25)

    pieces = (real_in, side_in, diag_in)

    def copy_of(kind, source, target):
        ref = pieces[kind]
        return pltpu.make_async_remote_copy(
            src_ref=ref.at[source],
            dst_ref=ref.at[source],
            send_sem=send_sem.at[kind, target],
            recv_sem=recv_sem.at[kind, source],
            device_id={"transpor": target},
            device_id_type=MESH,
        )

    early = {0: [(0, 3), (2, 3), (0, 2), (2, 2)], 3: [(0, 0), (1, 0), (0, 1), (1, 1)]}
    later = {
        0: [(1, 3), (1, 2), (1, 1)],
        1: [(0, 2), (2, 2), (0, 3), (2, 3), (0, 0), (2, 0), (1, 0), (1, 2), (1, 3)],
        2: [(0, 1), (2, 1), (1, 1), (0, 0), (2, 0), (1, 0), (0, 3), (2, 3), (1, 3)],
    }
    for source, what in early.items():

        @pl.when(x == source)
        def _():
            for kind, target in what:
                copy_of(kind, source, target).start()

    right = x < 2

    @pl.when(right)
    def _():
        copy_of(0, 3, 0).wait_recv()
        copy_of(1, 3, 0).wait_recv()
        matrix[0] = real_in[3]
        matrix[1] = side_in[3]

    @pl.when(x >= 2)
    def _():
        copy_of(0, 0, 3).wait_recv()
        copy_of(2, 0, 3).wait_recv()
        matrix[0] = real_in[0]
        matrix[1] = diagonal(diag_in[0][:1])

    for source, what in later.items():

        @pl.when(x == source)
        def _():
            for kind, target in what:
                copy_of(kind, source, target).start()

    @pl.loop(1, 8)
    def _(s):
        pl.semaphore_signal(line_sem, inc=1, device_id={"energy": row_peer(s)}, device_id_type=MESH)

    far_copy = pltpu.make_async_remote_copy(
        src_ref=near,
        dst_ref=far,
        send_sem=far_sem.at[0],
        recv_sem=far_sem.at[1],
        device_id={"transpor": 3 - x},
        device_id_type=MESH,
    )

    def set_coupling(slot, plain, source):
        @pl.when(plain)
        def _():
            coupling[slot] = side_in[source]

        @pl.when(jnp.logical_not(plain))
        def _():
            coupling[slot] = side_in[source].T

    def dressed(slot, gr, gi):
        h = coupling[slot]
        half = mm(h, jnp.concatenate([gr, gi], 1))
        both = mm(jnp.concatenate([half[:, :N], half[:, N:]], 0), h, ((1,), (1,)))
        return half, both[:N], both[N:]

    def stage(number, carry):
        inverse_r, inverse_i = invert(matrix[0], matrix[1])

        @pl.when(number == 0)
        def _():
            near[0] = inverse_r
            near[1] = inverse_i
            far_copy.start()

            @pl.when(right)
            def _():
                copy_of(0, 2, 0).wait_recv()
                copy_of(2, 2, 0).wait_recv()
                copy_of(1, 2, 0).wait_recv()
                set_coupling(0, right, 2)
                matrix[0] = real_in[2]
                matrix[1] = diagonal(diag_in[2][:1])

            @pl.when(x >= 2)
            def _():
                copy_of(0, 1, 3).wait_recv()
                copy_of(2, 1, 3).wait_recv()
                copy_of(1, 0, 3).wait_recv()
                set_coupling(0, right, 0)
                matrix[0] = real_in[1]
                matrix[1] = diagonal(diag_in[1][:1])

            _, sr, si = dressed(0, inverse_r, inverse_i)
            matrix[0] = matrix[0] - sr
            matrix[1] = matrix[1] - si

        @pl.when(number == 1)
        def _():
            @pl.when(x == 0)
            def _():
                copy_of(0, 1, 0).wait_recv()
                copy_of(2, 1, 0).wait_recv()
                copy_of(1, 1, 0).wait_recv()

            @pl.when(x == 1)
            def _():
                copy_of(1, 0, 1).wait_recv()

            @pl.when(x == 2)
            def _():
                copy_of(1, 1, 2).wait_recv()

            @pl.when(x == 3)
            def _():
                copy_of(0, 2, 3).wait_recv()
                copy_of(2, 2, 3).wait_recv()
                copy_of(1, 1, 3).wait_recv()
                copy_of(1, 2, 3).wait_recv()

            set_coupling(1, right, 1)

            @pl.when(right)
            def _():
                set_coupling(2, x >= 2, 0)
                matrix[0] = real_in[1]
                matrix[1] = diagonal(diag_in[1][:1])

            @pl.when(x >= 2)
            def _():
                set_coupling(2, x >= 2, 2)
                matrix[0] = real_in[2]
                matrix[1] = diagonal(diag_in[2][:1])

            _, sr, si = dressed(1, inverse_r, inverse_i)
            far_copy.wait_recv()
            half, tr, ti = dressed(2, far[0], far[1])
            lifted[...] = half
            matrix[0] = matrix[0] - (sr + tr)
            matrix[1] = matrix[1] - (si + ti)

        @pl.when(number == 2)
        def _():
            @pl.when((x == 1) | (x == 2))
            def _():
                own[0] = inverse_r
                own[1] = inverse_i

            @pl.when((x == 0) | (x == 3))
            def _():
                half = lifted[...]
                ur, ui = half[:, :N], half[:, N:]
                first = mm(inverse_r, half)
                second = mm(inverse_i, half)
                vr = first[:, :N] - second[:, N:]
                vi = first[:, N:] + second[:, :N]
                v = jnp.concatenate([vr, vi], 1)
                first = mm(ur, v, ((0,), (0,)))
                second = mm(ui, v, ((0,), (0,)))
                own[0] = far[0] + (first[:, :N] - second[:, N:])
                own[1] = far[1] + (first[:, N:] + second[:, :N])

        return carry

    lax.fori_loop(0, 3, stage, 0)

    save = pltpu.make_async_copy(own, green, green_sem)
    save.start()
    pl.semaphore_wait(line_sem, 7)

    def exchange(source, target, slot):
        def copy(s):
            other = lax.rem(e + s, NE)
            return pltpu.make_async_remote_copy(
                src_ref=source.at[:, pl.ds(other, 1), :],
                dst_ref=target.at[:, pl.ds(e, 1), :],
                send_sem=swap_sem.at[slot, 0],
                recv_sem=swap_sem.at[slot, 1],
                device_id={"energy": other},
                device_id_type=MESH,
            )

        @pl.loop(1, NE)
        def _(s):
            copy(s).start()

        pltpu.make_async_copy(
            source.at[:, pl.ds(e, 1), :], target.at[:, pl.ds(e, 1), :], swap_sem.at[slot, 1]
        ).start()
        pltpu.make_async_copy(source, target, swap_sem.at[slot, 1]).wait()

    def sent(source, target, slot):
        part = pl.ds(0, NE - 1)
        pltpu.make_async_copy(source.at[:, part, :], target.at[:, part, :], swap_sem.at[slot, 0]).wait()

    exchange(own, spread, 0)
    for copy in tables:
        copy.wait()

    values = jnp.concatenate([spread[0], spread[1]], 1)
    high, low = split2(values)
    spec = jnp.dot(forward_table[...], jnp.concatenate([high, low, high], 0), preferred_element_type=F32)
    a, cc = spec[:NE, :N], spec[:NE, N:]
    d, b = spec[NE:, :N], spec[NE:, N:]
    first_row = lax.broadcasted_iota(jnp.int32, (NE, N), 0) == 0
    upper, lower = a * a + cc * cc, b * b + d * d
    power = jnp.concatenate(
        [jnp.where(first_row, upper, upper + lower), jnp.where(first_row, lower, a * b - cc * d)], 0
    )
    high, low = split2(power)
    both = jnp.dot(backward_table[...], jnp.concatenate([high, low, high], 0), preferred_element_type=F32)
    sums[0] = both[:NE]
    sums[1] = both[NE:]
    exchange(sums, block, 1)
    finish = pltpu.make_async_copy(block, polar, table_sem.at[0])
    finish.start()

    sent(own, spread, 0)
    sent(sums, block, 1)
    far_copy.wait_send()
    for source in range(4):

        @pl.when(x == source)
        def _():
            for kind, target in early.get(source, []) + later.get(source, []):
                copy_of(kind, source, target).wait_send()

    save.wait()
    finish.wait()


def on_device(onsite, hopping, selfenergy, broadening):
    forward, backward = correlation_tables()
    forward, backward = jnp.asarray(forward), jnp.asarray(backward)
    whole = pl.BlockSpec(memory_space=pltpu.VMEM)
    left = pl.BlockSpec(memory_space=pl.ANY)
    pair = jax.ShapeDtypeStruct((2, N, N), F32)
    green, polar = pl.pallas_call(
        fused,
        out_shape=(pair, pair),
        in_specs=[whole, whole, whole, whole, left, left],
        out_specs=(left, left),
        scratch_shapes=[
            pltpu.VMEM((4, N, N), F32),
            pltpu.VMEM((4, N, N), F32),
            pltpu.VMEM((4, 8, N), F32),
            pltpu.VMEM((2, N, N), F32),
            pltpu.VMEM((2, N, N), F32),
            pltpu.VMEM((2, N, N), F32),
            pltpu.VMEM((2, N, N), F32),
            pltpu.VMEM((3, N, N), F32),
            pltpu.VMEM((N, 2 * N), F32),
            pltpu.VMEM((2, N, N), F32),
            pltpu.VMEM((2, NE, N), F32),
            pltpu.VMEM((2, NE, N), F32),
            pltpu.VMEM(forward.shape, BF16),
            pltpu.VMEM(backward.shape, BF16),
            pltpu.SemaphoreType.DMA((3, 4)),
            pltpu.SemaphoreType.DMA((3, 4)),
            pltpu.SemaphoreType.DMA((2,)),
            pltpu.SemaphoreType.DMA((2,)),
            pltpu.SemaphoreType.DMA((2, 2)),
            pltpu.SemaphoreType.DMA,
            pltpu.SemaphoreType.REGULAR,
        ],
        compiler_params=pltpu.CompilerParams(
            collective_id=0, has_side_effects=True, vmem_limit_bytes=48 * 2**20
        ),
    )(onsite[0], hopping[0], selfenergy[0, 0], broadening[0], forward, backward)
    return green[None, :, None], polar[None, :, None]


def solution(mesh):
    placed = (
        P("transpor", None, None),
        P("transpor", None, None),
        P("energy", "transpor", None, None),
        P("energy", "transpor", None),
    )
    return jax.shard_map(
        on_device,
        mesh=mesh,
        in_specs=placed,
        out_specs=(
            P("energy", None, "transpor", None, None),
            P("energy", None, "transpor", None, None),
        ),
        check_vma=False,
    )
```

```python
import jax
import jax.numpy as jnp
import numpy as np
from jax import lax
from jax.experimental import pallas as pl
from jax.experimental.pallas import tpu as pltpu
from jax.sharding import PartitionSpec as P

N = 128
NB = 8
NE = 128
ENERGY_LOW = -1.5
ENERGY_HIGH = 1.5
MESH = pl.DeviceIdType.MESH
F32 = jnp.float32
BF16 = jnp.bfloat16


def correlation_tables():
    freq = np.arange(NE)[:, None]
    time = np.arange(NE)[None, :]
    angle = 2.0 * np.pi * ((freq * time) % (2 * NE)) / (2 * NE)
    cosine, sine = np.cos(angle), np.sin(angle)
    alternate = np.where(np.arange(NE) % 2 == 0, 1.0, -1.0)
    lower = sine.copy()
    lower[0] = alternate
    forward = np.concatenate([cosine, lower], 0)
    weight = np.full((NE,), 2.0)
    weight[0] = 1.0
    scale = 1.0 / (2 * NE * NE)
    upper_right = np.zeros((NE, NE))
    upper_right[:, 0] = alternate
    backward = scale * np.block([[cosine.T * weight[None, :], upper_right], [np.zeros((NE, NE)), 4.0 * sine.T]])

    def halves(table):
        high = table.astype(np.float32).astype(BF16)
        low = (table - high.astype(np.float64)).astype(np.float32).astype(BF16)
        return high, low

    fh, fl = halves(forward)
    bh, bl = halves(backward)
    return np.concatenate([fh, fh, fl], 1), np.concatenate([bh, bh, bl], 1)


def split2(x):
    high = x.astype(BF16)
    return high, (x - high.astype(F32)).astype(BF16)


def split3(x):
    high = x.astype(BF16).astype(F32)
    rest = x - high
    middle = rest.astype(BF16).astype(F32)
    return high, middle, rest - middle


def lane_copy(x, column):
    return jnp.take_along_axis(x, jnp.full((NB, N), column, jnp.int32), axis=1)


def row_copy(x, row):
    return jnp.broadcast_to(x[row : row + 1, :], (NB, N))


def product(a, b):
    return a[0] * b[0] - a[1] * b[1], a[0] * b[1] + a[1] * b[0]


def total(terms):
    while len(terms) > 1:
        odd = [terms[-1]] if len(terms) % 2 else []
        terms = [terms[i] + terms[i + 1] for i in range(0, len(terms) - 1, 2)] + odd
    return terms[0]


def eliminate(panel, sub, lane, units, first):
    columns = [(lane_copy(panel[0], first + j), lane_copy(panel[1], first + j)) for j in range(NB)]
    active = (lane >= first) & (lane < first + NB)
    unit = jnp.where(lane == first + sub, 1.0, 0.0)
    rest = (jnp.where(active, unit, panel[0]), jnp.where(active, 0.0, panel[1]))
    for row in range(NB):
        column = columns[row]
        pivot = (row_copy(column[0], row), row_copy(column[1], row))
        over = 1.0 / (pivot[0] * pivot[0] + pivot[1] * pivot[1])
        less = (column[0] - units[row], column[1])
        if row + 1 < NB:
            x = columns[row + 1]
            line = (row_copy(x[0], row), row_copy(x[1], row))
            line = (pivot[0] * line[0] + pivot[1] * line[1], pivot[0] * line[1] - pivot[1] * line[0])
            step = product(less, line)
            columns[row + 1] = (x[0] - step[0] * over, x[1] - step[1] * over)
        factor = (less[0] * pivot[0] + less[1] * pivot[1], less[1] * pivot[0] - less[0] * pivot[1])
        factor = (factor[0] * over, factor[1] * over)

        def reduced(x):
            step = product(factor, (row_copy(x[0], row), row_copy(x[1], row)))
            return x[0] - step[0], x[1] - step[1]

        for j in range(row + 2, NB):
            columns[j] = reduced(columns[j])
        rest = reduced(rest)
    return rest


def stacked(left, right):
    ls = (split3(left[0]), split3(left[1]))
    ws = (split3(right[0]), split3(right[1]))
    lhs, rhs = [], []
    for a, b in ((0, 0), (0, 1), (1, 0), (1, 1), (0, 2), (2, 0)):
        lhs += [ls[0][a], ls[1][a]]
        rhs += [
            jnp.concatenate([ws[0][b], ws[1][b]], 1),
            jnp.concatenate([-ws[1][b], ws[0][b]], 1),
        ]
    return jnp.concatenate(lhs, 0), jnp.concatenate(rhs, 0)


def invert(matrix):
    count = N // NB
    lane = lax.broadcasted_iota(jnp.int32, (NB, N), 1)
    sub = lax.broadcasted_iota(jnp.int32, (NB, N), 0)
    units = [jnp.where(sub == row, 1.0, 0.0) for row in range(NB)]
    tiles = [(matrix[0, NB * k : NB * k + NB, :], matrix[1, NB * k : NB * k + NB, :]) for k in range(count)]
    panel = tiles[0]
    for k in range(count):
        first = NB * k
        active = (lane >= first) & (lane < first + NB)
        solved = eliminate(panel, sub, lane, units, first)
        done = lane < first
        left = (jnp.where(done, -panel[0], panel[0]), jnp.where(done, -panel[1], panel[1]))
        tiles[k] = solved
        if k + 1 < count:
            below = tiles[k + 1]
            terms = []
            for row in range(NB):
                factor = (lane_copy(below[0], first + row), lane_copy(below[1], first + row))
                terms.append(product(factor, (row_copy(solved[0], row), row_copy(solved[1], row))))
            panel = (
                jnp.where(active, 0.0, below[0]) - total([t[0] for t in terms]),
                jnp.where(active, 0.0, below[1]) - total([t[1] for t in terms]),
            )
            tiles[k + 1] = panel
        order = list(range(k + 2, count)) + list(range(k))
        lhs, rhs = stacked(left, (jnp.where(lane == first + sub, solved[0] + 1.0, solved[0]), solved[1]))
        lhs = lhs.T
        lhs = jnp.concatenate([lhs[NB * i : NB * i + NB] for i in order], 0)
        update = lax.dot_general(
            lhs, rhs, (((1,), (0,)), ((), ())), precision=lax.Precision.DEFAULT, preferred_element_type=F32
        )
        for place, i in enumerate(order):
            rows = slice(NB * place, NB * place + NB)
            tiles[i] = (tiles[i][0] - update[rows, :N], tiles[i][1] - update[rows, N:])
    return jnp.concatenate([t[0] for t in tiles], 0), jnp.concatenate([t[1] for t in tiles], 0)


def left3(x):
    high, low = split2(x)
    return jnp.concatenate([high, high, low], 1)


def right3(x, axis=0):
    high, low = split2(x)
    return jnp.concatenate([high, low, high], axis)


def dot3(a, b, dims=((1,), (0,))):
    return lax.dot_general(a, b, (dims, ((), ())), preferred_element_type=F32)


def fused(
    onsite_in,
    hopping_in,
    selfenergy_in,
    broadening_in,
    forward,
    backward,
    own,
    polar,
    onsite,
    hopping,
    selfenergy,
    broadening,
    turned,
    real_in,
    side_in,
    diag_in,
    near,
    far,
    matrix,
    lifted,
    spread,
    sums,
    forward_table,
    backward_table,
    send_sem,
    recv_sem,
    far_sem,
    input_sem,
    swap_sem,
    line_sem,
):
    x = lax.axis_index("transpor")
    e = lax.axis_index("energy")
    z, y, c = e // 16, lax.rem(e // 2, 8), lax.rem(e, 2)
    plane = z * 2 + c

    def plane_peer(s):
        i = lax.rem(plane + s, 16)
        return (i // 2) * 16 + y * 2 + lax.rem(i, 2)

    def row_peer(s):
        return z * 16 + lax.rem(y + s, 8) * 2 + c

    inputs = [
        pltpu.make_async_copy(source, target, input_sem.at[i])
        for i, (source, target) in enumerate(
            (
                (onsite_in, onsite),
                (selfenergy_in, selfenergy),
                (broadening_in, broadening),
                (hopping_in, hopping),
                (forward, forward_table),
                (backward, backward_table),
            )
        )
    ]
    for copy in inputs[:4]:
        copy.start()

    barrier = pltpu.get_barrier_semaphore()
    for s in range(1, 4):
        pl.semaphore_signal(barrier, inc=1, device_id={"transpor": lax.rem(x + s, 4)}, device_id_type=MESH)

    @pl.loop(1, 16)
    def _(s):
        pl.semaphore_signal(barrier, inc=1, device_id={"energy": plane_peer(s)}, device_id_type=MESH)

    @pl.loop(1, 8)
    def _(s):
        pl.semaphore_signal(barrier, inc=1, device_id={"energy": row_peer(s)}, device_id_type=MESH)

    level = ENERGY_LOW + (ENERGY_HIGH - ENERGY_LOW) * (e.astype(F32) + 0.5) / NE
    rows = lax.broadcasted_iota(jnp.int32, (N, N), 0)
    lanes = lax.broadcasted_iota(jnp.int32, (N, N), 1)
    unit = rows == lanes

    def diagonal(row):
        return jnp.where(unit, jnp.broadcast_to(row, (N, N)), 0.0)

    for copy in inputs[:4]:
        copy.wait()
    real_in[x] = jnp.where(unit, level, 0.0) - onsite[...] - selfenergy[...]
    diag_in[x] = jnp.broadcast_to(broadening[...], (8, N))

    @pl.when(x == 0)
    def _():
        side_in[0] = hopping[...].T

    @pl.when(x == 1)
    def _():
        side_in[1] = hopping[...]
        turned[...] = hopping[...].T

    @pl.when(x == 2)
    def _():
        side_in[2] = hopping[...]

    @pl.when(x == 3)
    def _():
        outgoing = hopping[...]
        side_in[3] = diagonal(broadening[...]) + dot3(left3(outgoing), right3(outgoing, 1), ((1,), (1,)))

    pl.semaphore_wait(barrier, 25)

    pieces = (real_in, side_in, diag_in)

    def copy_of(kind, source, target):
        ref = pieces[kind]
        return pltpu.make_async_remote_copy(
            src_ref=turned if kind == 1 and source == 1 and target > 1 else ref.at[source],
            dst_ref=ref.at[source],
            send_sem=send_sem.at[kind, target],
            recv_sem=recv_sem.at[kind, source],
            device_id={"transpor": target},
            device_id_type=MESH,
        )

    early = {0: [(0, 0, 2), (2, 0, 2), (0, 0, 3), (2, 0, 3)], 3: [(0, 3, 1), (1, 3, 1), (0, 3, 0), (1, 3, 0)]}
    later = {
        0: [(1, 0, 2), (1, 0, 3), (1, 0, 1)],
        1: [(2, 1, 3), (0, 1, 3), (2, 1, 2), (0, 1, 2), (1, 1, 0), (2, 1, 0), (0, 1, 0), (1, 1, 3), (1, 1, 2)],
        2: [(2, 2, 0), (0, 2, 0), (1, 2, 0), (2, 2, 1), (0, 2, 1), (1, 2, 1), (2, 2, 3), (0, 2, 3), (1, 2, 3)],
    }
    for source, what in early.items():

        @pl.when(x == source)
        def _():
            for item in what:
                copy_of(*item).start()

    right = x < 2
    left = x >= 2

    @pl.when(right)
    def _():
        copy_of(0, 3, 0).wait_recv()
        copy_of(1, 3, 0).wait_recv()
        matrix[0] = real_in[3]
        matrix[1] = side_in[3]

    @pl.when(left)
    def _():
        copy_of(2, 0, 3).wait_recv()
        copy_of(0, 0, 3).wait_recv()
        matrix[0] = real_in[0]
        matrix[1] = diagonal(diag_in[0][:1])

    for source, what in later.items():

        @pl.when(x == source)
        def _():
            for item in what:
                copy_of(*item).start()

    @pl.loop(1, 8)
    def _(s):
        pl.semaphore_signal(line_sem, inc=1, device_id={"energy": row_peer(s)}, device_id_type=MESH)

    for copy in inputs[4:]:
        copy.start()

    far_copy = pltpu.make_async_remote_copy(
        src_ref=near,
        dst_ref=far,
        send_sem=far_sem.at[0],
        recv_sem=far_sem.at[1],
        device_id={"transpor": 3 - x},
        device_id_type=MESH,
    )

    def dressed(h, gr, gi):
        half = dot3(left3(h), right3(jnp.concatenate([gr, gi], 1)))
        both = dot3(left3(jnp.concatenate([half[:, :N], half[:, N:]], 0)), right3(h, 1), ((1,), (1,)))
        return half, both[:N], both[N:]

    def stage(number, carry):
        inverse_r, inverse_i = invert(matrix)

        @pl.when(number == 0)
        def _():
            near[0] = inverse_r
            near[1] = inverse_i
            far_copy.start()

            @pl.when(right)
            def _():
                copy_of(2, 2, 0).wait_recv()
                copy_of(0, 2, 0).wait_recv()
                copy_of(1, 2, 0).wait_recv()

            @pl.when(left)
            def _():
                copy_of(2, 1, 3).wait_recv()
                copy_of(0, 1, 3).wait_recv()
                copy_of(1, 0, 3).wait_recv()

            block = jnp.where(right, 2, 1)
            _, sr, si = dressed(side_in[jnp.where(right, 2, 0)], inverse_r, inverse_i)
            matrix[0] = real_in[block] - sr
            matrix[1] = diagonal(diag_in[block][:1]) - si

        @pl.when(number == 1)
        def _():
            @pl.when(x == 0)
            def _():
                copy_of(1, 1, 0).wait_recv()
                copy_of(2, 1, 0).wait_recv()
                copy_of(0, 1, 0).wait_recv()

            @pl.when(x == 1)
            def _():
                copy_of(1, 0, 1).wait_recv()

            @pl.when(x == 2)
            def _():
                copy_of(1, 1, 2).wait_recv()

            @pl.when(x == 3)
            def _():
                copy_of(1, 1, 3).wait_recv()
                copy_of(2, 2, 3).wait_recv()
                copy_of(0, 2, 3).wait_recv()
                copy_of(1, 2, 3).wait_recv()

            block = jnp.where(right, 1, 2)
            _, sr, si = dressed(side_in[1], inverse_r, inverse_i)
            far_copy.wait_recv()
            half, tr, ti = dressed(side_in[jnp.where(right, 0, 2)], far[0], far[1])
            lifted[...] = half
            matrix[0] = real_in[block] - (sr + tr)
            matrix[1] = diagonal(diag_in[block][:1]) - (si + ti)

        @pl.when(number == 2)
        def _():
            @pl.when((x == 1) | (x == 2))
            def _():
                own[0] = inverse_r
                own[1] = inverse_i

            @pl.when((x == 0) | (x == 3))
            def _():
                half = lifted[...]
                four = dot3(left3(jnp.concatenate([inverse_r, inverse_i], 0)), right3(half))
                v = jnp.concatenate([four[:N, :N] - four[N:, N:], four[:N, N:] + four[N:, :N]], 1)
                four = dot3(left3(half.T), right3(v))
                own[0] = far[0] + (four[:N, :N] - four[N:, N:])
                own[1] = far[1] + (four[:N, N:] + four[N:, :N])

        return carry

    lax.fori_loop(0, 3, stage, 0)

    pl.semaphore_wait(line_sem, 7)

    def ordered(i):
        odd = lax.rem(i, 2)
        return 4 + (1 - odd) * (i // 2) - odd * ((i + 1) // 2)

    def exchange(source, target, slot):
        def copy(s):
            oz = lax.rem(z + ordered(s // 16), 8)
            oy = lax.rem(y + ordered(lax.rem(s // 2, 8)), 8)
            other = oz * 16 + oy * 2 + lax.rem(c + 1 - lax.rem(s, 2), 2)
            return pltpu.make_async_remote_copy(
                src_ref=source.at[:, pl.ds(other, 1), :],
                dst_ref=target.at[:, pl.ds(e, 1), :],
                send_sem=swap_sem.at[slot, 0],
                recv_sem=swap_sem.at[slot, 1],
                device_id={"energy": other},
                device_id_type=MESH,
            )

        @pl.loop(0, NE - 1)
        def _(s):
            copy(s).start()

        pltpu.make_async_copy(
            source.at[:, pl.ds(e, 1), :], target.at[:, pl.ds(e, 1), :], swap_sem.at[slot, 1]
        ).start()
        pltpu.make_async_copy(source, target, swap_sem.at[slot, 1]).wait()

    def sent(source, target, slot):
        part = pl.ds(0, NE - 1)
        pltpu.make_async_copy(source.at[:, part, :], target.at[:, part, :], swap_sem.at[slot, 0]).wait()

    exchange(own, spread, 0)
    for copy in inputs[4:]:
        copy.wait()

    values = jnp.concatenate([spread[0], spread[1]], 1)
    spec = dot3(forward_table[...], right3(values))
    a, cc = spec[:NE, :N], spec[:NE, N:]
    d, b = spec[NE:, :N], spec[NE:, N:]
    first_row = lax.broadcasted_iota(jnp.int32, (NE, N), 0) == 0
    upper, lower = a * a + cc * cc, b * b + d * d
    power = jnp.concatenate(
        [jnp.where(first_row, upper, upper + lower), jnp.where(first_row, lower, a * b - cc * d)], 0
    )
    both = dot3(backward_table[...], right3(power))
    sums[0] = both[:NE]
    sums[1] = both[NE:]
    exchange(sums, polar, 1)

    sent(own, spread, 0)
    sent(sums, polar, 1)
    far_copy.wait_send()
    for source in range(4):

        @pl.when(x == source)
        def _():
            for item in early.get(source, []) + later.get(source, []):
                copy_of(*item).wait_send()


def on_device(onsite, hopping, selfenergy, broadening):
    forward, backward = correlation_tables()
    forward, backward = jnp.asarray(forward), jnp.asarray(backward)
    whole = pl.BlockSpec(memory_space=pltpu.VMEM)
    stay = pl.BlockSpec(memory_space=pltpu.HBM)
    pair = jax.ShapeDtypeStruct((2, N, N), F32)
    green, polar = pl.pallas_call(
        fused,
        out_shape=(pair, pair),
        in_specs=[stay] * 6,
        out_specs=(whole, whole),
        scratch_shapes=[
            pltpu.VMEM((N, N), F32),
            pltpu.VMEM((N, N), F32),
            pltpu.VMEM((N, N), F32),
            pltpu.VMEM((1, N), F32),
            pltpu.VMEM((N, N), F32),
            pltpu.VMEM((4, N, N), F32),
            pltpu.VMEM((4, N, N), F32),
            pltpu.VMEM((4, 8, N), F32),
            pltpu.VMEM((2, N, N), F32),
            pltpu.VMEM((2, N, N), F32),
            pltpu.VMEM((2, N, N), F32),
            pltpu.VMEM((N, 2 * N), F32),
            pltpu.VMEM((2, NE, N), F32),
            pltpu.VMEM((2, NE, N), F32),
            pltpu.VMEM(forward.shape, BF16),
            pltpu.VMEM(backward.shape, BF16),
            pltpu.SemaphoreType.DMA((3, 4)),
            pltpu.SemaphoreType.DMA((3, 4)),
            pltpu.SemaphoreType.DMA((2,)),
            pltpu.SemaphoreType.DMA((6,)),
            pltpu.SemaphoreType.DMA((2, 2)),
            pltpu.SemaphoreType.REGULAR,
        ],
        compiler_params=pltpu.CompilerParams(
            collective_id=0, has_side_effects=True, vmem_limit_bytes=48 * 2**20
        ),
    )(
        *(
            pltpu.with_memory_space_constraint(array, pltpu.HBM)
            for array in (onsite[0], hopping[0], selfenergy[0, 0], broadening[0], forward, backward)
        )
    )
    return green[None, :, None], polar[None, :, None]


def solution(mesh):
    placed = (
        P("transpor", None, None),
        P("transpor", None, None),
        P("energy", "transpor", None, None),
        P("energy", "transpor", None),
    )
    return jax.shard_map(
        on_device,
        mesh=mesh,
        in_specs=placed,
        out_specs=(
            P("energy", None, "transpor", None, None),
            P("energy", None, "transpor", None, None),
        ),
        check_vma=False,
    )
```

```python
import jax
import jax.numpy as jnp
import numpy as np
from jax import lax
from jax.experimental import pallas as pl
from jax.experimental.pallas import tpu as pltpu
from jax.sharding import PartitionSpec as P

N = 128
NB = 8
NE = 128
ENERGY_LOW = -1.5
ENERGY_HIGH = 1.5
MESH = pl.DeviceIdType.MESH
F32 = jnp.float32
BF16 = jnp.bfloat16


def correlation_tables():
    freq = np.arange(NE)[:, None]
    time = np.arange(NE)[None, :]
    angle = 2.0 * np.pi * ((freq * time) % (2 * NE)) / (2 * NE)
    cosine, sine = np.cos(angle), np.sin(angle)
    alternate = np.where(np.arange(NE) % 2 == 0, 1.0, -1.0)
    lower = sine.copy()
    lower[0] = alternate
    forward = np.concatenate([cosine, lower], 0)
    weight = np.full((NE,), 2.0)
    weight[0] = 1.0
    scale = 1.0 / (2 * NE * NE)
    upper_right = np.zeros((NE, NE))
    upper_right[:, 0] = alternate
    backward = scale * np.block([[cosine.T * weight[None, :], upper_right], [np.zeros((NE, NE)), 4.0 * sine.T]])

    def halves(table):
        high = table.astype(np.float32).astype(BF16)
        low = (table - high.astype(np.float64)).astype(np.float32).astype(BF16)
        return high, low

    fh, fl = halves(forward)
    bh, bl = halves(backward)
    return np.concatenate([fh, fh, fl], 1), np.concatenate([bh, bh, bl], 1)


def split2(x):
    high = x.astype(BF16)
    return high, (x - high.astype(F32)).astype(BF16)


def split3(x):
    high = x.astype(BF16).astype(F32)
    rest = x - high
    middle = rest.astype(BF16).astype(F32)
    return high, middle, rest - middle


def lane_copy(x, column):
    return jnp.take_along_axis(x, jnp.full((NB, N), column, jnp.int32), axis=1)


def row_copy(x, row):
    return jnp.broadcast_to(x[row : row + 1, :], (NB, N))


def product(a, b):
    return a[0] * b[0] - a[1] * b[1], a[0] * b[1] + a[1] * b[0]


def total(terms):
    while len(terms) > 1:
        odd = [terms[-1]] if len(terms) % 2 else []
        terms = [terms[i] + terms[i + 1] for i in range(0, len(terms) - 1, 2)] + odd
    return terms[0]


def eliminate(panel, sub, lane, units, first):
    columns = [(lane_copy(panel[0], first + j), lane_copy(panel[1], first + j)) for j in range(NB)]
    active = (lane >= first) & (lane < first + NB)
    unit = jnp.where(lane == first + sub, 1.0, 0.0)
    rest = (jnp.where(active, unit, panel[0]), jnp.where(active, 0.0, panel[1]))
    for row in range(NB):
        column = columns[row]
        pivot = (row_copy(column[0], row), row_copy(column[1], row))
        over = 1.0 / (pivot[0] * pivot[0] + pivot[1] * pivot[1])
        less = (column[0] - units[row], column[1])
        if row + 1 < NB:
            x = columns[row + 1]
            line = (row_copy(x[0], row), row_copy(x[1], row))
            line = (pivot[0] * line[0] + pivot[1] * line[1], pivot[0] * line[1] - pivot[1] * line[0])
            step = product(less, line)
            columns[row + 1] = (x[0] - step[0] * over, x[1] - step[1] * over)
        factor = (less[0] * pivot[0] + less[1] * pivot[1], less[1] * pivot[0] - less[0] * pivot[1])
        factor = (factor[0] * over, factor[1] * over)

        def reduced(x):
            step = product(factor, (row_copy(x[0], row), row_copy(x[1], row)))
            return x[0] - step[0], x[1] - step[1]

        for j in range(row + 2, NB):
            columns[j] = reduced(columns[j])
        rest = reduced(rest)
    return rest


def stacked(left, right):
    ls = (split3(left[0]), split3(left[1]))
    ws = (split3(right[0]), split3(right[1]))
    lhs, rhs = [], []
    for a, b in ((0, 0), (0, 1), (1, 0), (1, 1), (0, 2), (2, 0)):
        lhs += [ls[0][a], ls[1][a]]
        rhs += [
            jnp.concatenate([ws[0][b], ws[1][b]], 1),
            jnp.concatenate([-ws[1][b], ws[0][b]], 1),
        ]
    return jnp.concatenate(lhs, 0), jnp.concatenate(rhs, 0)


def invert(matrix):
    count = N // NB
    lane = lax.broadcasted_iota(jnp.int32, (NB, N), 1)
    sub = lax.broadcasted_iota(jnp.int32, (NB, N), 0)
    units = [jnp.where(sub == row, 1.0, 0.0) for row in range(NB)]
    tiles = [(matrix[0, NB * k : NB * k + NB, :], matrix[1, NB * k : NB * k + NB, :]) for k in range(count)]
    panel = tiles[0]
    for k in range(count):
        first = NB * k
        active = (lane >= first) & (lane < first + NB)
        solved = eliminate(panel, sub, lane, units, first)
        done = lane < first
        left = (jnp.where(done, -panel[0], panel[0]), jnp.where(done, -panel[1], panel[1]))
        tiles[k] = solved
        if k + 1 < count:
            below = tiles[k + 1]
            terms = []
            for row in range(NB):
                factor = (lane_copy(below[0], first + row), lane_copy(below[1], first + row))
                terms.append(product(factor, (row_copy(solved[0], row), row_copy(solved[1], row))))
            panel = (
                jnp.where(active, 0.0, below[0]) - total([t[0] for t in terms]),
                jnp.where(active, 0.0, below[1]) - total([t[1] for t in terms]),
            )
            tiles[k + 1] = panel
        order = list(range(k + 2, count)) + list(range(k))
        lhs, rhs = stacked(left, (jnp.where(lane == first + sub, solved[0] + 1.0, solved[0]), solved[1]))
        lhs = lhs.T
        lhs = jnp.concatenate([lhs[NB * i : NB * i + NB] for i in order], 0)
        update = lax.dot_general(
            lhs, rhs, (((1,), (0,)), ((), ())), precision=lax.Precision.DEFAULT, preferred_element_type=F32
        )
        for place, i in enumerate(order):
            rows = slice(NB * place, NB * place + NB)
            tiles[i] = (tiles[i][0] - update[rows, :N], tiles[i][1] - update[rows, N:])
    return jnp.concatenate([t[0] for t in tiles], 0), jnp.concatenate([t[1] for t in tiles], 0)


def left3(x):
    high, low = split2(x)
    return jnp.concatenate([high, high, low], 1)


def right3(x, axis=0):
    high, low = split2(x)
    return jnp.concatenate([high, low, high], axis)


def dot3(a, b, dims=((1,), (0,))):
    return lax.dot_general(a, b, (dims, ((), ())), preferred_element_type=F32)


def fused(
    onsite_in,
    hopping_in,
    selfenergy_in,
    broadening_in,
    forward,
    backward,
    own,
    polar,
    onsite,
    hopping,
    selfenergy,
    broadening,
    turned,
    real_in,
    side_in,
    diag_in,
    near,
    far,
    matrix,
    lifted,
    spread,
    sums,
    forward_table,
    backward_table,
    send_sem,
    recv_sem,
    far_sem,
    input_sem,
    swap_sem,
    line_sem,
):
    x = lax.axis_index("transpor")
    e = lax.axis_index("energy")
    z, y, c = e // 16, lax.rem(e // 2, 8), lax.rem(e, 2)
    plane = z * 2 + c

    def plane_peer(s):
        i = lax.rem(plane + s, 16)
        return (i // 2) * 16 + y * 2 + lax.rem(i, 2)

    def row_peer(s):
        return z * 16 + lax.rem(y + s, 8) * 2 + c

    inputs = [
        pltpu.make_async_copy(source, target, input_sem.at[i])
        for i, (source, target) in enumerate(
            (
                (onsite_in, onsite),
                (selfenergy_in, selfenergy),
                (broadening_in, broadening),
                (hopping_in, hopping),
                (forward, forward_table),
                (backward, backward_table),
            )
        )
    ]
    for copy in inputs[:4]:
        copy.start()

    barrier = pltpu.get_barrier_semaphore()
    for s in range(1, 4):
        pl.semaphore_signal(barrier, inc=1, device_id={"transpor": lax.rem(x + s, 4)}, device_id_type=MESH)

    @pl.loop(1, 16)
    def _(s):
        pl.semaphore_signal(barrier, inc=1, device_id={"energy": plane_peer(s)}, device_id_type=MESH)

    @pl.loop(1, 8)
    def _(s):
        pl.semaphore_signal(barrier, inc=1, device_id={"energy": row_peer(s)}, device_id_type=MESH)

    level = ENERGY_LOW + (ENERGY_HIGH - ENERGY_LOW) * (e.astype(F32) + 0.5) / NE
    rows = lax.broadcasted_iota(jnp.int32, (N, N), 0)
    lanes = lax.broadcasted_iota(jnp.int32, (N, N), 1)
    unit = rows == lanes

    def diagonal(row):
        return jnp.where(unit, jnp.broadcast_to(row, (N, N)), 0.0)

    for copy in inputs[:4]:
        copy.wait()
    real_in[x] = jnp.where(unit, level, 0.0) - onsite[...] - selfenergy[...]
    diag_in[x] = jnp.broadcast_to(broadening[...], (8, N))

    @pl.when(x == 0)
    def _():
        side_in[0] = hopping[...].T

    @pl.when(x == 1)
    def _():
        side_in[1] = hopping[...]
        turned[...] = hopping[...].T

    @pl.when(x == 2)
    def _():
        side_in[2] = hopping[...]

    @pl.when(x == 3)
    def _():
        outgoing = hopping[...]
        side_in[3] = diagonal(broadening[...]) + dot3(left3(outgoing), right3(outgoing, 1), ((1,), (1,)))

    pl.semaphore_wait(barrier, 25)

    pieces = (real_in, side_in, diag_in)

    def copy_of(kind, source, target):
        ref = pieces[kind]
        return pltpu.make_async_remote_copy(
            src_ref=turned if kind == 1 and source == 1 and target > 1 else ref.at[source],
            dst_ref=ref.at[source],
            send_sem=send_sem.at[kind, target],
            recv_sem=recv_sem.at[kind, source],
            device_id={"transpor": target},
            device_id_type=MESH,
        )

    early = {0: [(0, 0, 2), (2, 0, 2), (0, 0, 3), (2, 0, 3)], 3: [(0, 3, 1), (1, 3, 1), (0, 3, 0), (1, 3, 0)]}
    later = {
        0: [(1, 0, 2), (1, 0, 3), (1, 0, 1)],
        1: [(2, 1, 3), (0, 1, 3), (2, 1, 2), (0, 1, 2), (1, 1, 0), (2, 1, 0), (0, 1, 0), (1, 1, 3), (1, 1, 2)],
        2: [(2, 2, 0), (0, 2, 0), (1, 2, 0), (2, 2, 1), (0, 2, 1), (1, 2, 1), (2, 2, 3), (0, 2, 3), (1, 2, 3)],
    }
    for source, what in early.items():

        @pl.when(x == source)
        def _():
            for item in what:
                copy_of(*item).start()

    right = x < 2
    left = x >= 2

    @pl.when(right)
    def _():
        copy_of(0, 3, 0).wait_recv()
        copy_of(1, 3, 0).wait_recv()
        matrix[0] = real_in[3]
        matrix[1] = side_in[3]

    @pl.when(left)
    def _():
        copy_of(2, 0, 3).wait_recv()
        copy_of(0, 0, 3).wait_recv()
        matrix[0] = real_in[0]
        matrix[1] = diagonal(diag_in[0][:1])

    for source, what in later.items():

        @pl.when(x == source)
        def _():
            for item in what:
                copy_of(*item).start()

    @pl.loop(1, 8)
    def _(s):
        pl.semaphore_signal(line_sem, inc=1, device_id={"energy": row_peer(s)}, device_id_type=MESH)

    for copy in inputs[4:]:
        copy.start()

    far_copy = pltpu.make_async_remote_copy(
        src_ref=near,
        dst_ref=far,
        send_sem=far_sem.at[0],
        recv_sem=far_sem.at[1],
        device_id={"transpor": 3 - x},
        device_id_type=MESH,
    )

    def dressed(h, gr, gi):
        half = dot3(left3(h), right3(jnp.concatenate([gr, gi], 1)))
        both = dot3(left3(jnp.concatenate([half[:, :N], half[:, N:]], 0)), right3(h, 1), ((1,), (1,)))
        return half, both[:N], both[N:]

    def stage(number, carry):
        inverse_r, inverse_i = invert(matrix)

        @pl.when(number == 0)
        def _():
            near[0] = inverse_r
            near[1] = inverse_i
            far_copy.start()

            @pl.when(right)
            def _():
                copy_of(2, 2, 0).wait_recv()
                copy_of(0, 2, 0).wait_recv()
                copy_of(1, 2, 0).wait_recv()

            @pl.when(left)
            def _():
                copy_of(2, 1, 3).wait_recv()
                copy_of(0, 1, 3).wait_recv()
                copy_of(1, 0, 3).wait_recv()

            block = jnp.where(right, 2, 1)
            _, sr, si = dressed(side_in[jnp.where(right, 2, 0)], inverse_r, inverse_i)
            matrix[0] = real_in[block] - sr
            matrix[1] = diagonal(diag_in[block][:1]) - si

        @pl.when(number == 1)
        def _():
            @pl.when(x == 0)
            def _():
                copy_of(1, 1, 0).wait_recv()
                copy_of(2, 1, 0).wait_recv()
                copy_of(0, 1, 0).wait_recv()

            @pl.when(x == 1)
            def _():
                copy_of(1, 0, 1).wait_recv()

            @pl.when(x == 2)
            def _():
                copy_of(1, 1, 2).wait_recv()

            @pl.when(x == 3)
            def _():
                copy_of(1, 1, 3).wait_recv()
                copy_of(2, 2, 3).wait_recv()
                copy_of(0, 2, 3).wait_recv()
                copy_of(1, 2, 3).wait_recv()

            block = jnp.where(right, 1, 2)
            _, sr, si = dressed(side_in[1], inverse_r, inverse_i)
            far_copy.wait_recv()
            half, tr, ti = dressed(side_in[jnp.where(right, 0, 2)], far[0], far[1])
            lifted[...] = half
            matrix[0] = real_in[block] - (sr + tr)
            matrix[1] = diagonal(diag_in[block][:1]) - (si + ti)

        @pl.when(number == 2)
        def _():
            @pl.when((x == 1) | (x == 2))
            def _():
                own[0] = inverse_r
                own[1] = inverse_i

            @pl.when((x == 0) | (x == 3))
            def _():
                half = lifted[...]
                four = dot3(left3(jnp.concatenate([inverse_r, inverse_i], 0)), right3(half))
                v = jnp.concatenate([four[:N, :N] - four[N:, N:], four[:N, N:] + four[N:, :N]], 1)
                four = dot3(left3(half.T), right3(v))
                own[0] = far[0] + (four[:N, :N] - four[N:, N:])
                own[1] = far[1] + (four[:N, N:] + four[N:, :N])

        return carry

    lax.fori_loop(0, 3, stage, 0)

    pl.semaphore_wait(line_sem, 7)

    steps_z = [lax.rem(z + i, 8) * 16 for i in range(8)]
    steps_y = [lax.rem(y + i, 8) * 2 for i in range(8)]
    steps_c = [c, 1 - c]
    order = [(i, j, k) for i in range(8) for j in range(8) for k in range(2)][1:]
    order.sort(key=lambda o: -(min(o[0], 8 - o[0]) + min(o[1], 8 - o[1])))

    def exchange(source, target, slot):
        for i, j, k in order:
            other = steps_z[i] + steps_y[j] + steps_c[k]
            pltpu.make_async_remote_copy(
                src_ref=source.at[:, pl.ds(other, 1), :],
                dst_ref=target.at[:, pl.ds(e, 1), :],
                send_sem=swap_sem.at[slot, 0],
                recv_sem=swap_sem.at[slot, 1],
                device_id={"energy": other},
                device_id_type=MESH,
            ).start()
        pltpu.make_async_copy(
            source.at[:, pl.ds(e, 1), :], target.at[:, pl.ds(e, 1), :], swap_sem.at[slot, 1]
        ).start()
        pltpu.make_async_copy(source, target, swap_sem.at[slot, 1]).wait()

    def sent(source, target, slot):
        part = pl.ds(0, NE - 1)
        pltpu.make_async_copy(source.at[:, part, :], target.at[:, part, :], swap_sem.at[slot, 0]).wait()

    exchange(own, spread, 0)
    for copy in inputs[4:]:
        copy.wait()

    values = jnp.concatenate([spread[0], spread[1]], 1)
    spec = dot3(forward_table[...], right3(values))
    a, cc = spec[:NE, :N], spec[:NE, N:]
    d, b = spec[NE:, :N], spec[NE:, N:]
    first_row = lax.broadcasted_iota(jnp.int32, (NE, N), 0) == 0
    upper, lower = a * a + cc * cc, b * b + d * d
    power = jnp.concatenate(
        [jnp.where(first_row, upper, upper + lower), jnp.where(first_row, lower, a * b - cc * d)], 0
    )
    both = dot3(backward_table[...], right3(power))
    sums[0] = both[:NE]
    sums[1] = both[NE:]
    exchange(sums, polar, 1)

    sent(own, spread, 0)
    sent(sums, polar, 1)
    far_copy.wait_send()
    for source in range(4):

        @pl.when(x == source)
        def _():
            for item in early.get(source, []) + later.get(source, []):
                copy_of(*item).wait_send()


def on_device(onsite, hopping, selfenergy, broadening):
    forward, backward = correlation_tables()
    forward, backward = jnp.asarray(forward), jnp.asarray(backward)
    whole = pl.BlockSpec(memory_space=pltpu.VMEM)
    stay = pl.BlockSpec(memory_space=pltpu.HBM)
    pair = jax.ShapeDtypeStruct((2, N, N), F32)
    green, polar = pl.pallas_call(
        fused,
        out_shape=(pair, pair),
        in_specs=[stay] * 6,
        out_specs=(whole, whole),
        scratch_shapes=[
            pltpu.VMEM((N, N), F32),
            pltpu.VMEM((N, N), F32),
            pltpu.VMEM((N, N), F32),
            pltpu.VMEM((1, N), F32),
            pltpu.VMEM((N, N), F32),
            pltpu.VMEM((4, N, N), F32),
            pltpu.VMEM((4, N, N), F32),
            pltpu.VMEM((4, 8, N), F32),
            pltpu.VMEM((2, N, N), F32),
            pltpu.VMEM((2, N, N), F32),
            pltpu.VMEM((2, N, N), F32),
            pltpu.VMEM((N, 2 * N), F32),
            pltpu.VMEM((2, NE, N), F32),
            pltpu.VMEM((2, NE, N), F32),
            pltpu.VMEM(forward.shape, BF16),
            pltpu.VMEM(backward.shape, BF16),
            pltpu.SemaphoreType.DMA((3, 4)),
            pltpu.SemaphoreType.DMA((3, 4)),
            pltpu.SemaphoreType.DMA((2,)),
            pltpu.SemaphoreType.DMA((6,)),
            pltpu.SemaphoreType.DMA((2, 2)),
            pltpu.SemaphoreType.REGULAR,
        ],
        compiler_params=pltpu.CompilerParams(
            collective_id=0, has_side_effects=True, vmem_limit_bytes=48 * 2**20
        ),
    )(
        *(
            pltpu.with_memory_space_constraint(array, pltpu.HBM)
            for array in (onsite[0], hopping[0], selfenergy[0, 0], broadening[0], forward, backward)
        )
    )
    return green[None, :, None], polar[None, :, None]


def solution(mesh):
    placed = (
        P("transpor", None, None),
        P("transpor", None, None),
        P("energy", "transpor", None, None),
        P("energy", "transpor", None),
    )
    return jax.shard_map(
        on_device,
        mesh=mesh,
        in_specs=placed,
        out_specs=(
            P("energy", None, "transpor", None, None),
            P("energy", None, "transpor", None, None),
        ),
        check_vma=False,
    )
```

```python
import jax
import jax.numpy as jnp
import numpy as np
from jax import lax
from jax.experimental import pallas as pl
from jax.experimental.pallas import tpu as pltpu
from jax.sharding import PartitionSpec as P

N = 128
NB = 8
NE = 128
ENERGY_LOW = -1.5
ENERGY_HIGH = 1.5
MESH = pl.DeviceIdType.MESH
F32 = jnp.float32
BF16 = jnp.bfloat16


def correlation_tables():
    freq = np.arange(NE)[:, None]
    time = np.arange(NE)[None, :]
    angle = 2.0 * np.pi * ((freq * time) % (2 * NE)) / (2 * NE)
    cosine, sine = np.cos(angle), np.sin(angle)
    alternate = np.where(np.arange(NE) % 2 == 0, 1.0, -1.0)
    lower = sine.copy()
    lower[0] = alternate
    forward = np.concatenate([cosine, lower], 0)
    weight = np.full((NE,), 2.0)
    weight[0] = 1.0
    scale = 1.0 / (2 * NE * NE)
    upper_right = np.zeros((NE, NE))
    upper_right[:, 0] = alternate
    backward = scale * np.block([[cosine.T * weight[None, :], upper_right], [np.zeros((NE, NE)), 4.0 * sine.T]])

    def halves(table):
        high = table.astype(np.float32).astype(BF16)
        low = (table - high.astype(np.float64)).astype(np.float32).astype(BF16)
        return high, low

    fh, fl = halves(forward)
    bh, bl = halves(backward)
    return np.concatenate([fh, fh, fl], 1), np.concatenate([bh, bh, bl], 1)


def split2(x):
    high = x.astype(BF16)
    return high, (x - high.astype(F32)).astype(BF16)


def split3(x):
    high = x.astype(BF16).astype(F32)
    rest = x - high
    middle = rest.astype(BF16).astype(F32)
    return high, middle, rest - middle


def lane_copy(x, column):
    return jnp.take_along_axis(x, jnp.full((NB, N), column, jnp.int32), axis=1)


def row_copy(x, row):
    return jnp.broadcast_to(x[row : row + 1, :], (NB, N))


def product(a, b):
    return a[0] * b[0] - a[1] * b[1], a[0] * b[1] + a[1] * b[0]


def total(terms):
    while len(terms) > 1:
        odd = [terms[-1]] if len(terms) % 2 else []
        terms = [terms[i] + terms[i + 1] for i in range(0, len(terms) - 1, 2)] + odd
    return terms[0]


def eliminate(panel, sub, lane, units, first):
    columns = [(lane_copy(panel[0], first + j), lane_copy(panel[1], first + j)) for j in range(NB)]
    active = (lane >= first) & (lane < first + NB)
    unit = jnp.where(lane == first + sub, 1.0, 0.0)
    rest = (jnp.where(active, unit, panel[0]), jnp.where(active, 0.0, panel[1]))
    for row in range(NB):
        column = columns[row]
        pivot = (row_copy(column[0], row), row_copy(column[1], row))
        over = 1.0 / (pivot[0] * pivot[0] + pivot[1] * pivot[1])
        less = (column[0] - units[row], column[1])
        if row + 1 < NB:
            x = columns[row + 1]
            line = (row_copy(x[0], row), row_copy(x[1], row))
            line = (pivot[0] * line[0] + pivot[1] * line[1], pivot[0] * line[1] - pivot[1] * line[0])
            step = product(less, line)
            columns[row + 1] = (x[0] - step[0] * over, x[1] - step[1] * over)
        factor = (less[0] * pivot[0] + less[1] * pivot[1], less[1] * pivot[0] - less[0] * pivot[1])
        factor = (factor[0] * over, factor[1] * over)

        def reduced(x):
            step = product(factor, (row_copy(x[0], row), row_copy(x[1], row)))
            return x[0] - step[0], x[1] - step[1]

        for j in range(row + 2, NB):
            columns[j] = reduced(columns[j])
        rest = reduced(rest)
    return rest


def stacked(left, right):
    ls = (split3(left[0]), split3(left[1]))
    ws = (split3(right[0]), split3(right[1]))
    lhs, rhs = [], []
    for a, b in ((0, 0), (0, 1), (1, 0), (1, 1), (0, 2), (2, 0)):
        lhs += [ls[0][a], ls[1][a]]
        rhs += [
            jnp.concatenate([ws[0][b], ws[1][b]], 1),
            jnp.concatenate([-ws[1][b], ws[0][b]], 1),
        ]
    return jnp.concatenate(lhs, 0), jnp.concatenate(rhs, 0)


def invert(matrix):
    count = N // NB
    lane = lax.broadcasted_iota(jnp.int32, (NB, N), 1)
    sub = lax.broadcasted_iota(jnp.int32, (NB, N), 0)
    units = [jnp.where(sub == row, 1.0, 0.0) for row in range(NB)]
    tiles = [(matrix[0, NB * k : NB * k + NB, :], matrix[1, NB * k : NB * k + NB, :]) for k in range(count)]
    panel = tiles[0]
    for k in range(count):
        first = NB * k
        active = (lane >= first) & (lane < first + NB)
        solved = eliminate(panel, sub, lane, units, first)
        done = lane < first
        left = (jnp.where(done, -panel[0], panel[0]), jnp.where(done, -panel[1], panel[1]))
        tiles[k] = solved
        if k + 1 < count:
            below = tiles[k + 1]
            terms = []
            for row in range(NB):
                factor = (lane_copy(below[0], first + row), lane_copy(below[1], first + row))
                terms.append(product(factor, (row_copy(solved[0], row), row_copy(solved[1], row))))
            panel = (
                jnp.where(active, 0.0, below[0]) - total([t[0] for t in terms]),
                jnp.where(active, 0.0, below[1]) - total([t[1] for t in terms]),
            )
            tiles[k + 1] = panel
        order = list(range(k + 2, count)) + list(range(k))
        lhs, rhs = stacked(left, (jnp.where(lane == first + sub, solved[0] + 1.0, solved[0]), solved[1]))
        lhs = lhs.T
        lhs = jnp.concatenate([lhs[NB * i : NB * i + NB] for i in order], 0)
        update = lax.dot_general(
            lhs, rhs, (((1,), (0,)), ((), ())), precision=lax.Precision.DEFAULT, preferred_element_type=F32
        )
        for place, i in enumerate(order):
            rows = slice(NB * place, NB * place + NB)
            tiles[i] = (tiles[i][0] - update[rows, :N], tiles[i][1] - update[rows, N:])
    return jnp.concatenate([t[0] for t in tiles], 0), jnp.concatenate([t[1] for t in tiles], 0)


def left3(x):
    high, low = split2(x)
    return jnp.concatenate([high, high, low], 1)


def right3(x, axis=0):
    high, low = split2(x)
    return jnp.concatenate([high, low, high], axis)


def dot3(a, b, dims=((1,), (0,))):
    return lax.dot_general(a, b, (dims, ((), ())), preferred_element_type=F32)


def fused(
    onsite_in,
    hopping_in,
    selfenergy_in,
    broadening_in,
    forward,
    backward,
    own,
    polar,
    onsite,
    hopping,
    selfenergy,
    broadening,
    turned,
    real_in,
    side_in,
    diag_in,
    near,
    far,
    matrix,
    lifted,
    packed,
    spread,
    sums,
    block,
    forward_table,
    backward_table,
    send_sem,
    recv_sem,
    far_sem,
    input_sem,
    swap_sem,
    line_sem,
):
    x = lax.axis_index("transpor")
    e = lax.axis_index("energy")
    z, y, c = e // 16, lax.rem(e // 2, 8), lax.rem(e, 2)
    plane = z * 2 + c

    def plane_peer(s):
        i = lax.rem(plane + s, 16)
        return (i // 2) * 16 + y * 2 + lax.rem(i, 2)

    def row_peer(s):
        return z * 16 + lax.rem(y + s, 8) * 2 + c

    inputs = [
        pltpu.make_async_copy(source, target, input_sem.at[i])
        for i, (source, target) in enumerate(
            (
                (onsite_in, onsite),
                (selfenergy_in, selfenergy),
                (broadening_in, broadening),
                (hopping_in, hopping),
                (forward, forward_table),
                (backward, backward_table),
            )
        )
    ]
    for copy in inputs[:4]:
        copy.start()

    barrier = pltpu.get_barrier_semaphore()
    for s in range(1, 4):
        pl.semaphore_signal(barrier, inc=1, device_id={"transpor": lax.rem(x + s, 4)}, device_id_type=MESH)

    @pl.loop(1, 16)
    def _(s):
        pl.semaphore_signal(barrier, inc=1, device_id={"energy": plane_peer(s)}, device_id_type=MESH)

    @pl.loop(1, 8)
    def _(s):
        pl.semaphore_signal(barrier, inc=1, device_id={"energy": row_peer(s)}, device_id_type=MESH)

    level = ENERGY_LOW + (ENERGY_HIGH - ENERGY_LOW) * (e.astype(F32) + 0.5) / NE
    rows = lax.broadcasted_iota(jnp.int32, (N, N), 0)
    lanes = lax.broadcasted_iota(jnp.int32, (N, N), 1)
    unit = rows == lanes

    def diagonal(row):
        return jnp.where(unit, jnp.broadcast_to(row, (N, N)), 0.0)

    for copy in inputs[:4]:
        copy.wait()
    real_in[x] = jnp.where(unit, level, 0.0) - onsite[...] - selfenergy[...]
    diag_in[x] = jnp.broadcast_to(broadening[...], (8, N))

    @pl.when(x == 0)
    def _():
        side_in[0] = hopping[...].T

    @pl.when(x == 1)
    def _():
        side_in[1] = hopping[...]
        turned[...] = hopping[...].T

    @pl.when(x == 2)
    def _():
        side_in[2] = hopping[...]

    @pl.when(x == 3)
    def _():
        outgoing = hopping[...]
        side_in[3] = diagonal(broadening[...]) + dot3(left3(outgoing), right3(outgoing, 1), ((1,), (1,)))

    pl.semaphore_wait(barrier, 25)

    pieces = (real_in, side_in, diag_in)

    def copy_of(kind, source, target):
        ref = pieces[kind]
        return pltpu.make_async_remote_copy(
            src_ref=turned if kind == 1 and source == 1 and target > 1 else ref.at[source],
            dst_ref=ref.at[source],
            send_sem=send_sem.at[kind, target],
            recv_sem=recv_sem.at[kind, source],
            device_id={"transpor": target},
            device_id_type=MESH,
        )

    early = {0: [(0, 0, 2), (2, 0, 2), (0, 0, 3), (2, 0, 3)], 3: [(0, 3, 1), (1, 3, 1), (0, 3, 0), (1, 3, 0)]}
    later = {
        0: [(1, 0, 2), (1, 0, 3), (1, 0, 1)],
        1: [(2, 1, 3), (0, 1, 3), (2, 1, 2), (0, 1, 2), (1, 1, 0), (2, 1, 0), (0, 1, 0), (1, 1, 3), (1, 1, 2)],
        2: [(2, 2, 0), (0, 2, 0), (1, 2, 0), (2, 2, 1), (0, 2, 1), (1, 2, 1), (2, 2, 3), (0, 2, 3), (1, 2, 3)],
    }
    for source, what in early.items():

        @pl.when(x == source)
        def _():
            for item in what:
                copy_of(*item).start()

    right = x < 2
    left = x >= 2

    @pl.when(right)
    def _():
        copy_of(0, 3, 0).wait_recv()
        copy_of(1, 3, 0).wait_recv()
        matrix[0] = real_in[3]
        matrix[1] = side_in[3]

    @pl.when(left)
    def _():
        copy_of(2, 0, 3).wait_recv()
        copy_of(0, 0, 3).wait_recv()
        matrix[0] = real_in[0]
        matrix[1] = diagonal(diag_in[0][:1])

    for source, what in later.items():

        @pl.when(x == source)
        def _():
            for item in what:
                copy_of(*item).start()

    @pl.loop(1, 8)
    def _(s):
        pl.semaphore_signal(line_sem, inc=1, device_id={"energy": row_peer(s)}, device_id_type=MESH)

    for copy in inputs[4:]:
        copy.start()

    far_copy = pltpu.make_async_remote_copy(
        src_ref=near,
        dst_ref=far,
        send_sem=far_sem.at[0],
        recv_sem=far_sem.at[1],
        device_id={"transpor": 3 - x},
        device_id_type=MESH,
    )

    def dressed(h, gr, gi):
        half = dot3(left3(h), right3(jnp.concatenate([gr, gi], 1)))
        both = dot3(left3(jnp.concatenate([half[:, :N], half[:, N:]], 0)), right3(h, 1), ((1,), (1,)))
        return half, both[:N], both[N:]

    def stage(number, carry):
        inverse_r, inverse_i = invert(matrix)

        @pl.when(number == 0)
        def _():
            near[0] = inverse_r
            near[1] = inverse_i
            far_copy.start()

            @pl.when(right)
            def _():
                copy_of(2, 2, 0).wait_recv()
                copy_of(0, 2, 0).wait_recv()
                copy_of(1, 2, 0).wait_recv()

            @pl.when(left)
            def _():
                copy_of(2, 1, 3).wait_recv()
                copy_of(0, 1, 3).wait_recv()
                copy_of(1, 0, 3).wait_recv()

            block = jnp.where(right, 2, 1)
            _, sr, si = dressed(side_in[jnp.where(right, 2, 0)], inverse_r, inverse_i)
            matrix[0] = real_in[block] - sr
            matrix[1] = diagonal(diag_in[block][:1]) - si

        @pl.when(number == 1)
        def _():
            @pl.when(x == 0)
            def _():
                copy_of(1, 1, 0).wait_recv()
                copy_of(2, 1, 0).wait_recv()
                copy_of(0, 1, 0).wait_recv()

            @pl.when(x == 1)
            def _():
                copy_of(1, 0, 1).wait_recv()

            @pl.when(x == 2)
            def _():
                copy_of(1, 1, 2).wait_recv()

            @pl.when(x == 3)
            def _():
                copy_of(1, 1, 3).wait_recv()
                copy_of(2, 2, 3).wait_recv()
                copy_of(0, 2, 3).wait_recv()
                copy_of(1, 2, 3).wait_recv()

            block = jnp.where(right, 1, 2)
            _, sr, si = dressed(side_in[1], inverse_r, inverse_i)
            far_copy.wait_recv()
            half, tr, ti = dressed(side_in[jnp.where(right, 0, 2)], far[0], far[1])
            lifted[...] = half
            matrix[0] = real_in[block] - (sr + tr)
            matrix[1] = diagonal(diag_in[block][:1]) - (si + ti)

        @pl.when(number == 2)
        def _():
            @pl.when((x == 1) | (x == 2))
            def _():
                own[0] = inverse_r
                own[1] = inverse_i

            @pl.when((x == 0) | (x == 3))
            def _():
                half = lifted[...]
                four = dot3(left3(jnp.concatenate([inverse_r, inverse_i], 0)), right3(half))
                v = jnp.concatenate([four[:N, :N] - four[N:, N:], four[:N, N:] + four[N:, :N]], 1)
                four = dot3(left3(half.T), right3(v))
                own[0] = far[0] + (four[:N, :N] - four[N:, N:])
                own[1] = far[1] + (four[:N, N:] + four[N:, :N])

        return carry

    lax.fori_loop(0, 3, stage, 0)

    pl.semaphore_wait(line_sem, 7)

    half = N // 2
    tall = lax.broadcasted_iota(jnp.int32, (half, N), 0)
    wide = lax.broadcasted_iota(jnp.int32, (half, N), 1)
    low = wide < half
    across = jnp.where(low, wide, wide - half)

    def turn(v):
        return pltpu.roll(v, half, 1)

    top_r, top_i, end_r, end_i = own[0, :half], own[1, :half], own[0, half:], own[1, half:]
    head = jnp.where(low, top_r, turn(top_i))
    tail = jnp.where(low, turn(end_r), end_i)
    packed[1] = jnp.where(low, turn(top_r), top_i)
    packed[2] = jnp.where(across >= tall, head, tail)
    middle = jnp.sum(jnp.where(across == tall, tail, 0.0), 0, keepdims=True)
    packed[0, half - 8 :] = jnp.broadcast_to(middle, (8, N))

    at_z = [lax.rem(z + i, 8) for i in range(8)]
    at_y = [lax.rem(y + i, 8) * 2 for i in range(8)]
    at_c = [c, 1 - c]
    upper_z = [k // 4 for k in at_z]

    def hops(o):
        return min(o[0], 8 - o[0]) + min(o[1], 8 - o[1])

    def rank(o):
        return at_z[o[0]] * 16 + at_y[o[1]] + at_c[o[2]]

    def row_of(o):
        return lax.rem(at_z[o[0]], 4) * 16 + lax.rem(at_y[o[1]] + 8 * upper_z[o[0]], 16) + at_c[o[2]]

    order = [(i, j, k) for i in range(8) for j in range(8) for k in range(2)][1:]
    order.sort(key=lambda o: -hops(o))
    mine = row_of((0, 0, 0))
    last = half - 1
    keepers = (3 * 16 + 7 * 2 + 1, 7 * 16 + 3 * 2 + 1)
    keeps = (e == keepers[0]) | (e == keepers[1])

    extras = [
        pltpu.make_async_remote_copy(
            src_ref=packed.at[0, pl.ds(last, 1), :],
            dst_ref=spread.at[0, pl.ds(e, 1), :],
            send_sem=swap_sem.at[2 + i, 0],
            recv_sem=swap_sem.at[2, 1],
            device_id={"energy": keeper},
            device_id_type=MESH,
        )
        for i, keeper in enumerate(keepers)
    ]
    for extra, keeper in zip(extras, keepers):

        @pl.when(e != keeper)
        def _():
            extra.start()

    pair = pl.ds(1, 2)
    for o in order:
        pltpu.make_async_remote_copy(
            src_ref=packed.at[pair, pl.ds(row_of(o), 1), :],
            dst_ref=spread.at[pair, pl.ds(e, 1), :],
            send_sem=swap_sem.at[0, 0],
            recv_sem=swap_sem.at[0, 1],
            device_id={"energy": rank(o)},
            device_id_type=MESH,
        ).start()
    pltpu.make_async_copy(
        packed.at[pair, pl.ds(mine, 1), :], spread.at[pair, pl.ds(e, 1), :], swap_sem.at[0, 1]
    ).start()
    pltpu.make_async_copy(sums.at[pair], spread.at[pair], swap_sem.at[0, 1]).wait()

    @pl.when(keeps)
    def _():
        pltpu.make_async_copy(
            packed.at[0, pl.ds(last, 1), :], spread.at[0, pl.ds(e, 1), :], swap_sem.at[2, 1]
        ).start()
        pltpu.make_async_copy(sums.at[0], spread.at[0], swap_sem.at[2, 1]).wait()

    @pl.when(jnp.logical_not(keeps))
    def _():
        spread[0] = jnp.zeros((NE, N), F32)

    for copy in inputs[4:]:
        copy.wait()

    values = jnp.concatenate([spread[0], spread[1], spread[2]], 1)
    spec = dot3(forward_table[...], right3(values))
    first_row = lax.broadcasted_iota(jnp.int32, (NE, N), 0) == 0
    left_lanes = lax.broadcasted_iota(jnp.int32, (NE, N), 1) < half
    powers = []
    for part in range(3):
        upper, lower = spec[:NE, N * part : N * part + N], spec[NE:, N * part : N * part + N]
        square, lower_square = upper * upper, lower * lower
        even = jnp.where(first_row, square, square + lower_square)
        cross = upper * turn(lower)
        odd = jnp.where(first_row, lower_square + turn(lower_square), cross - turn(cross))
        powers.append(jnp.concatenate([even + turn(even), odd], 0))
    both = dot3(backward_table[...], right3(jnp.concatenate(powers, 1)))
    for part in range(3):
        real, imag = both[:NE, N * part : N * part + N], both[NE:, N * part : N * part + N]
        sums[part] = jnp.where(left_lanes, real, -imag)

    def give(near_planes, tie_planes):
        for o in order:
            if hops(o) > 4:
                continue
            planes = near_planes if hops(o) < 4 else tie_planes
            pltpu.make_async_remote_copy(
                src_ref=sums.at[planes, pl.ds(rank(o), 1), :],
                dst_ref=block.at[planes, pl.ds(mine, 1), :],
                send_sem=swap_sem.at[1, 0] if hops(o) < 4 else swap_sem.at[3, 1],
                recv_sem=swap_sem.at[1, 1],
                device_id={"energy": rank(o)},
                device_id_type=MESH,
            ).start()
        pltpu.make_async_copy(
            sums.at[near_planes, pl.ds(e, 1), :], block.at[near_planes, pl.ds(mine, 1), :], swap_sem.at[1, 1]
        ).start()

    @pl.when(jnp.logical_not(keeps))
    def _():
        give(pair, pl.ds(1 + upper_z[0], 1))

    @pl.when(e == keepers[0])
    def _():
        give(pl.ds(0, 3), pl.ds(0, 2))

    @pl.when(e == keepers[1])
    def _():
        give(pl.ds(0, 3), pl.ds(2, 1))

    part = pl.ds(0, (2 * half + 1) // 3)
    pltpu.make_async_copy(packed.at[:, part, :], block.at[:, part, :], swap_sem.at[1, 1]).wait()

    corner, wedge = block[1], block[2]
    middle = block[0, last:]
    corner_t, wedge_t = corner.T, wedge.T
    for part in range(2):
        flat = wedge if part == 0 else turn(wedge)
        side = turn(corner) if part == 0 else corner
        line = jnp.broadcast_to(middle, (half, N))
        line = line if part == 0 else turn(line)
        mirror = wedge_t[half * part : half * part + half]
        mirror = jnp.concatenate([mirror, mirror], 1)
        under = corner_t[half * part : half * part + half]
        under = jnp.concatenate([under, under], 1)
        first = jnp.where(across >= tall, flat, mirror)
        final = jnp.where(across < tall, flat, jnp.where(across > tall, mirror, line))
        polar[part, :half] = jnp.where(low, first, side)
        polar[part, half:] = jnp.where(low, under, turn(final))

    for extra, keeper in zip(extras, keepers):

        @pl.when(e != keeper)
        def _():
            extra.wait_send()

    part = pl.ds(0, NE - 1)
    pltpu.make_async_copy(sums.at[pair, part, :], spread.at[pair, part, :], swap_sem.at[0, 0]).wait()

    near_part = pl.ds(0, sum(hops(o) < 4 for o in order))
    tie_part = pl.ds(0, sum(hops(o) == 4 for o in order))

    def given(near_count, tie_count):
        for planes, part, sem in (
            (pl.ds(0, near_count), near_part, swap_sem.at[1, 0]),
            (pl.ds(0, tie_count), tie_part, swap_sem.at[3, 1]),
        ):
            pltpu.make_async_copy(sums.at[planes, part, :], spread.at[planes, part, :], sem).wait()

    @pl.when(jnp.logical_not(keeps))
    def _():
        given(2, 1)

    @pl.when(e == keepers[0])
    def _():
        given(3, 2)

    @pl.when(e == keepers[1])
    def _():
        given(3, 1)

    far_copy.wait_send()
    for source in range(4):

        @pl.when(x == source)
        def _():
            for item in early.get(source, []) + later.get(source, []):
                copy_of(*item).wait_send()


def on_device(onsite, hopping, selfenergy, broadening):
    forward, backward = correlation_tables()
    forward, backward = jnp.asarray(forward), jnp.asarray(backward)
    whole = pl.BlockSpec(memory_space=pltpu.VMEM)
    stay = pl.BlockSpec(memory_space=pltpu.HBM)
    pair = jax.ShapeDtypeStruct((2, N, N), F32)
    green, polar = pl.pallas_call(
        fused,
        out_shape=(pair, pair),
        in_specs=[stay] * 6,
        out_specs=(whole, whole),
        scratch_shapes=[
            pltpu.VMEM((N, N), F32),
            pltpu.VMEM((N, N), F32),
            pltpu.VMEM((N, N), F32),
            pltpu.VMEM((1, N), F32),
            pltpu.VMEM((N, N), F32),
            pltpu.VMEM((4, N, N), F32),
            pltpu.VMEM((4, N, N), F32),
            pltpu.VMEM((4, 8, N), F32),
            pltpu.VMEM((2, N, N), F32),
            pltpu.VMEM((2, N, N), F32),
            pltpu.VMEM((2, N, N), F32),
            pltpu.VMEM((N, 2 * N), F32),
            pltpu.VMEM((3, N // 2, N), F32),
            pltpu.VMEM((3, NE, N), F32),
            pltpu.VMEM((3, NE, N), F32),
            pltpu.VMEM((3, N // 2, N), F32),
            pltpu.VMEM(forward.shape, BF16),
            pltpu.VMEM(backward.shape, BF16),
            pltpu.SemaphoreType.DMA((3, 4)),
            pltpu.SemaphoreType.DMA((3, 4)),
            pltpu.SemaphoreType.DMA((2,)),
            pltpu.SemaphoreType.DMA((6,)),
            pltpu.SemaphoreType.DMA((4, 2)),
            pltpu.SemaphoreType.REGULAR,
        ],
        compiler_params=pltpu.CompilerParams(
            collective_id=0, has_side_effects=True, vmem_limit_bytes=48 * 2**20
        ),
    )(
        *(
            pltpu.with_memory_space_constraint(array, pltpu.HBM)
            for array in (onsite[0], hopping[0], selfenergy[0, 0], broadening[0], forward, backward)
        )
    )
    return green[None, :, None], polar[None, :, None]


def solution(mesh):
    placed = (
        P("transpor", None, None),
        P("transpor", None, None),
        P("energy", "transpor", None, None),
        P("energy", "transpor", None),
    )
    return jax.shard_map(
        on_device,
        mesh=mesh,
        in_specs=placed,
        out_specs=(
            P("energy", None, "transpor", None, None),
            P("energy", None, "transpor", None, None),
        ),
        check_vma=False,
    )
```
